32 devices in a mesh: groups: 2 (over y), aux: 4 (over z), pts: 2 (over x), rep: 2 (over core).
Axes of the slice: x: 2, y: 2, z: 4, core: 2. Of those that a mesh axis runs over, the one named last changes fastest.
Arguments:
- density_slab: bfloat16 [32, 1024, 1024], P('groups', 'aux', 'rep'), parts along dimension 0, may hold values from -0.005859375 to 0.005859375
- orbitals: bfloat16 [2048, 8192], P(('groups', 'rep'), 'pts'), parts along dimension 0, may hold values from -6 to 6
Outputs:
- rhs_share: float32 [16384, 8192], P(('groups', 'pts'), ('aux', 'rep')), parts along dimension 0
The draws below stay inside these ranges and needn't reach their ends.
There are 2 independent parts, one for each index of `groups`. The reference program is written for one: setup_inputs(seed, part) draws one part's arguments, and reference() takes and returns one part's arrays. A program takes and returns all parts, laid end to end along the dimension named above; each array names one. Nothing has to cross between parts.
All inputs are finite; a program needn't handle non-finite values.
Results may differ from the reference program's by a relative error of at most 0.0003.
Values may be sent and summed in bfloat16 or wider, within the bound.
A program may use at most 64 MiB of HBM per device.

```python
import jax
import jax.numpy as jnp
from jax import lax

NBF = 1024
NPTS = 8192
AUX = 16


def block_levels(own_key, extent, shards, smallest, largest):
    level = 1.0
    for dim, parts in shards:
        heights = jax.random.uniform(jax.random.fold_in(jax.random.fold_in(own_key, 6), dim), (parts,), jnp.float32, smallest / len(shards), largest / len(shards))
        level = level * jnp.repeat(jnp.exp(heights), extent[dim] // parts).reshape((-1,) + (1,) * (len(extent) - 1 - dim))
    return level


def noise(own_key, extent, deviation, limit, split=(), dtype=jnp.bfloat16):
    gain = block_levels(own_key, extent, split, -0.22, 0.18) if split else 1.0
    values = jax.random.normal(own_key, extent, jnp.float32) * deviation * gain
    return jnp.minimum(jnp.maximum(values, -limit), limit).astype(dtype)


def setup_inputs(seed: int = 0, part: int = 0) -> dict:
    seeds = jax.random.split(jax.random.key(seed), 3)
    part_splits = jax.random.split(jax.random.fold_in(seeds[2], part), 3)
    density_slab = noise(part_splits[0], (AUX, NBF, NBF), (NBF * NBF) ** -0.5, 0.005859375, ((1, 4), (2, 2)))
    orbitals = noise(part_splits[1], (NBF, NPTS), 1.0, 6.0, ((0, 2), (1, 2)))
    return dict(density_slab=density_slab, orbitals=orbitals)


def reference(density_slab, orbitals):
    colloc = orbitals.astype(jnp.float32)

    def one_slice(slab):
        contracted = jnp.dot(slab, orbitals, preferred_element_type=jnp.float32)
        return jnp.sum(colloc * contracted, axis=0)

    weights = lax.map(one_slice, density_slab)
    total = jnp.dot(weights.T, weights, precision=lax.Precision.HIGHEST, preferred_element_type=jnp.float32)
    return total / jnp.float32(AUX)
```

```python
import functools

import jax
import jax.numpy as jnp
from jax import lax
from jax.experimental import pallas as pl
from jax.experimental.pallas import tpu as pltpu
from jax.sharding import PartitionSpec as P


MESH = pl.DeviceIdType.MESH
HEAD = 2


def split(w):
    high = w.astype(jnp.bfloat16)
    return high, (w - high.astype(jnp.float32)).astype(jnp.bfloat16)


def plan(own_pts, block):
    unit = max(128, block // 2)
    chunks = [(t, unit) for t in range(0, own_pts - unit, unit)]
    fine = unit // 2 if unit >= 256 else unit
    tail = [(t, fine) for t in range(own_pts - unit, own_pts, fine)]
    return unit, chunks, tail


def partial_weights(d_ref, q_ref, p_ref, out_ref, t, width, ready=None):
    n_k, n_p, n_q = d_ref.shape
    group = max(1, 512 // n_p)
    there = slice(t, t + width)
    q_rows = q_ref[:, there]
    p_rows = p_ref[:, there].astype(jnp.float32)
    for k in range(0, n_k, group):
        if ready is not None:
            ready(k // group)
        lhs = d_ref[k : k + group].reshape(group * n_p, n_q)
        c = jnp.dot(lhs, q_rows, preferred_element_type=jnp.float32)
        for j in range(group):
            term = c[j * n_p : (j + 1) * n_p] * p_rows
            out_ref[k + j : k + j + 1, there] = jnp.sum(term, axis=0, keepdims=True)


def load_kernel(
    unit, d_hbm, orb_hbm, d_ref, q_ref, p_ref, part_ref, d_sem, q_sem, p_sem, ps_sem
):
    n_k, n_p, n_q = d_hbm.shape
    pieces = orb_hbm.shape[1] // unit
    group = max(1, 512 // n_p)
    a, r = lax.axis_index("aux"), lax.axis_index("rep")
    first = a * n_p
    owner, offset = first // n_q, pl.multiple_of(first % n_q, n_p)

    def cols(g):
        return pl.ds(g * unit, unit)

    def d_copy(i):
        ks = pl.ds(i * group, group)
        return pltpu.make_async_copy(d_hbm.at[ks], d_ref.at[ks], d_sem.at[i])

    def q_copy(g):
        return pltpu.make_async_copy(
            orb_hbm.at[:, cols(g)], q_ref.at[:, cols(g)], q_sem.at[g]
        )

    def p_local(g):
        return pltpu.make_async_copy(
            orb_hbm.at[pl.ds(offset, n_p), cols(g)], p_ref.at[:, cols(g)], p_sem.at[g]
        )

    def p_remote(g):
        return pltpu.make_async_remote_copy(
            orb_hbm.at[pl.ds(offset, n_p), cols(g)], p_ref.at[:, cols(g)],
            ps_sem.at[g], p_sem.at[g],
            device_id={"rep": 1 - r}, device_id_type=MESH,
        )

    barrier = pltpu.get_barrier_semaphore()
    pl.semaphore_signal(barrier, inc=1, device_id={"rep": 1 - r}, device_id_type=MESH)
    q_copy(0).start()
    for i in range(n_k // group):
        d_copy(i).start()

    @pl.when(owner == r)
    def _():
        p_local(0).start()

    pl.semaphore_wait(barrier, 1)

    @pl.when(owner == r)
    def _():
        for g in range(pieces):
            p_remote(g).start()

    for g in range(1, pieces):
        q_copy(g).start()

    @pl.when(owner == r)
    def _():
        for g in range(1, pieces):
            p_local(g).start()

    def arrive(g):
        q_copy(g).wait()

        @pl.when(owner == r)
        def _():
            p_local(g).wait()

        @pl.when(owner != r)
        def _():
            p_remote(g).wait_recv()

    for g in range(HEAD):
        arrive(g)
        partial_weights(
            d_ref, q_ref, p_ref, part_ref, g * unit, unit,
            (lambda i: d_copy(i).wait()) if g == 0 else None,
        )
    for g in range(HEAD, pieces):
        arrive(g)

    @pl.when(owner == r)
    def _():
        for g in range(pieces):
            p_remote(g).wait_send()


def share_kernel(
    sizes, chunks, tail, d_ref, q_ref, p_ref, head_ref, left_ref, right_ref,
    part, pair, z_buf, tot, cols_buf, bc, xd,
    pair_send, pair_recv, z_send, z_recv, core_send, core_recv, x_send, x_recv,
    bc_send, bc_recv, xd_send, xd_recv,
):
    n_aux, n_pts, n_rep, block = sizes
    n_k = d_ref.shape[0]
    half = n_k // n_rep
    members = n_aux * n_rep
    blocks = members // n_pts
    a, x, r = lax.axis_index("aux"), lax.axis_index("pts"), lax.axis_index("rep")
    me = a * n_rep + r
    home = me // blocks
    mine = me % blocks
    n_main = len(chunks)
    every = chunks + tail
    begin = tail[0][0]
    own_half = pl.ds(pl.multiple_of(r * half, half), half)
    other_half = pl.ds(pl.multiple_of((1 - r) * half, half), half)

    def member(j):
        return {"aux": j // n_rep, "rep": j % n_rep}

    def span(c):
        return pl.ds(*every[c])

    def tail_span(c):
        return pl.ds(every[c][0] - begin, every[c][1])

    def terms(c):
        return head_ref if c < HEAD else part

    def pair_copy(c):
        return pltpu.make_async_remote_copy(
            terms(c).at[other_half, span(c)], pair.at[:, span(c)],
            pair_send.at[c], pair_recv.at[c],
            device_id={"rep": 1 - r}, device_id_type=MESH,
        )

    def z_copy(c, step):
        return pltpu.make_async_remote_copy(
            z_buf.at[a, :, span(c)], z_buf.at[a, :, span(c)],
            z_send.at[c, step - 1], z_recv.at[c, step - 1],
            device_id={"aux": (a + step) % n_aux}, device_id_type=MESH,
        )

    def z_arrival(c, step):
        source = (a + n_aux - step) % n_aux
        return pltpu.make_async_remote_copy(
            z_buf.at[source, :, span(c)], z_buf.at[source, :, span(c)],
            z_send.at[c, step - 1], z_recv.at[c, step - 1],
            device_id={"aux": (a + step) % n_aux}, device_id_type=MESH,
        )

    def core_copy(c, which):
        return pltpu.make_async_remote_copy(
            tot.at[which, :, span(c)], tot.at[which, :, span(c)],
            core_send.at[c], core_recv.at[c],
            device_id={"rep": 1 - r}, device_id_type=MESH,
        )

    def x_target(c, step):
        target = member(x * blocks + every[c][0] // block)
        target["pts"] = (x + step) % n_pts
        return target

    def x_copy(c, which, step):
        within = pl.ds(every[c][0] % block, every[c][1])
        return pltpu.make_async_remote_copy(
            tot.at[which, :, span(c)], cols_buf.at[which, :, within],
            x_send.at[c, step - 1], x_recv.at[c, which],
            device_id=x_target(c, step), device_id_type=MESH,
        )

    def bc_copy(c, step):
        return pltpu.make_async_remote_copy(
            bc.at[me, :, tail_span(c)], bc.at[me, :, tail_span(c)],
            bc_send.at[c - n_main, step - 1], bc_recv.at[c - n_main, step - 1],
            device_id=member((me + step) % members), device_id_type=MESH,
        )

    def bc_arrival(c, step):
        source = (me + members - step) % members
        return pltpu.make_async_remote_copy(
            bc.at[source, :, tail_span(c)], bc.at[source, :, tail_span(c)],
            bc_send.at[c - n_main, step - 1], bc_recv.at[c - n_main, step - 1],
            device_id=member((me + step) % members), device_id_type=MESH,
        )

    def xd_copy(c, slot, step):
        return pltpu.make_async_remote_copy(
            bc.at[slot, :, tail_span(c)], xd.at[slot, :, tail_span(c)],
            xd_send.at[c - n_main, step - 1], xd_recv.at[c - n_main, slot],
            device_id=x_target(c, step), device_id_type=MESH,
        )

    barrier = pltpu.get_barrier_semaphore()
    for step in range(1, members):
        pl.semaphore_signal(
            barrier, inc=1, device_id=member((me + step) % members), device_id_type=MESH
        )

    @pl.when(home != x)
    def _():
        for i in range(members):
            source = {"aux": i // n_rep, "rep": i % n_rep, "pts": home}
            pl.semaphore_signal(barrier, inc=1, device_id=source, device_id_type=MESH)

    def pair_sum(c):
        pair_copy(c).wait_recv()
        return terms(c)[own_half, span(c)] + pair[:, span(c)]

    def exchange(c):
        if c < n_main:
            z_buf[a, :, span(c)] = pair_sum(c)
            for step in range(1, n_aux):
                z_copy(c, step).start()
        else:
            bc[me, :, tail_span(c)] = pair_sum(c)
            for step in range(1, members):
                bc_copy(c, step).start()
            for step in range(1, n_pts):
                xd_copy(c, me, step).start()

    def finish(c):
        for step in range(1, n_aux):
            z_arrival(c, step).wait_recv()
        total = z_buf[0, :, span(c)]
        for i in range(1, n_aux):
            total = total + z_buf[i, :, span(c)]
        tot[r, :, span(c)] = total
        core_copy(c, r).start()

        @pl.when((x * blocks + every[c][0] // block) // n_rep == a)
        def _():
            for step in range(1, n_pts):
                x_copy(c, r, step).start()

    def place(c, w):
        high, low = split(w)
        left_ref[0:n_k, span(c)] = high
        left_ref[n_k : 2 * n_k, span(c)] = high
        left_ref[2 * n_k : 3 * n_k, span(c)] = low

    def assemble(c):
        core_copy(c, 1 - r).wait_recv()
        place(c, jnp.concatenate([tot[i, :, span(c)] for i in range(n_rep)], axis=0))

    def gathered(ref, c):
        sums = []
        for i in range(n_rep):
            total = ref[i, :, tail_span(c)]
            for j in range(1, n_aux):
                total = total + ref[j * n_rep + i, :, tail_span(c)]
            sums.append(total)
        return sums

    n = len(every)
    for c in range(HEAD, n):
        partial_weights(d_ref, q_ref, p_ref, part, *every[c])
        if c == HEAD:
            pl.semaphore_wait(barrier, members - 1 + (n_pts - 1) * blocks)
            for i in range(HEAD + 1):
                pair_copy(i).start()
        else:
            pair_copy(c).start()
            for i in range(HEAD + 1) if c == HEAD + 1 else (c - 1,):
                exchange(i)
    exchange(n - 1)

    for c in range(n_main):
        finish(c)
    for c in range(n_main):
        assemble(c)

    for c in range(n_main, n):
        for step in range(1, members):
            bc_arrival(c, step).wait_recv()
        sums = gathered(bc, c)
        for i in range(n_rep):
            tot[i, :, span(c)] = sums[i]
        place(c, jnp.concatenate(sums, axis=0))

    @pl.when(home == x)
    def _():
        there = pl.ds(pl.multiple_of(mine * block, block), block)
        for i in range(n_rep):
            cols_buf[i] = tot[i, :, there]

    for b in range(blocks):

        @pl.when((home != x) & (mine == b))
        def _(b=b):
            for c in range(n):
                if every[c][0] // block != b:
                    continue
                if c < n_main:
                    for i in range(n_rep):
                        x_copy(c, i, 1).wait_recv()
                else:
                    for j in range(members):
                        xd_copy(c, j, 1).wait_recv()
                    sums = gathered(xd, c)
                    for i in range(n_rep):
                        cols_buf[i, :, pl.ds(every[c][0] % block, every[c][1])] = sums[i]

    high, low = split(jnp.concatenate([cols_buf[i] for i in range(n_rep)], axis=0))
    right_ref[0:n_k, :] = high
    right_ref[n_k : 2 * n_k, :] = low
    right_ref[2 * n_k : 3 * n_k, :] = high

    for c in range(n):
        pair_copy(c).wait_send()
        if c < n_main:
            for step in range(1, n_aux):
                z_copy(c, step).wait_send()
            core_copy(c, r).wait_send()

            @pl.when((x * blocks + every[c][0] // block) // n_rep == a)
            def _(c=c):
                for step in range(1, n_pts):
                    x_copy(c, r, step).wait_send()
        else:
            for step in range(1, members):
                bc_copy(c, step).wait_send()
            for step in range(1, n_pts):
                xd_copy(c, me, step).wait_send()


def factors(density, orbitals):
    n_k, n_p, n_q = density.shape
    own_pts = orbitals.shape[1]
    n_aux, n_pts, n_rep = (lax.axis_size(name) for name in ("aux", "pts", "rep"))
    members = n_aux * n_rep
    block = own_pts * n_pts // members
    half = n_k // n_rep
    unit, chunks, tail = plan(own_pts, block)
    n_main, n_tail = len(chunks), len(tail)
    n = n_main + n_tail
    group = max(1, 512 // n_p)
    dma = pltpu.SemaphoreType.DMA
    f32, bf16 = jnp.float32, jnp.bfloat16
    vmem = pl.BlockSpec(memory_space=pltpu.VMEM)
    d, q, p, head = pl.pallas_call(
        functools.partial(load_kernel, unit),
        in_specs=[pl.BlockSpec(memory_space=pl.ANY)] * 2,
        out_specs=[vmem] * 4,
        out_shape=[
            pltpu.VMEM((n_k, n_p, n_q), bf16),
            pltpu.VMEM((n_q, own_pts), bf16),
            pltpu.VMEM((n_p, own_pts), bf16),
            pltpu.VMEM((n_k, HEAD * unit), f32),
        ],
        scratch_shapes=[
            dma((n_k // group,)),
            dma((own_pts // unit,)),
            dma((own_pts // unit,)),
            dma((own_pts // unit,)),
        ],
        compiler_params=pltpu.CompilerParams(
            collective_id=0, has_side_effects=True, vmem_limit_bytes=51 << 20
        ),
    )(density, orbitals)
    return pl.pallas_call(
        functools.partial(share_kernel, (n_aux, n_pts, n_rep, block), chunks, tail),
        in_specs=[vmem] * 4,
        out_specs=[vmem] * 2,
        out_shape=[
            pltpu.VMEM((3 * n_k, own_pts), bf16),
            pltpu.VMEM((3 * n_k, block), bf16),
        ],
        scratch_shapes=[
            pltpu.VMEM((n_k, own_pts), f32),
            pltpu.VMEM((half, own_pts), f32),
            pltpu.VMEM((n_aux, half, own_pts), f32),
            pltpu.VMEM((n_rep, half, own_pts), f32),
            pltpu.VMEM((n_rep, half, block), f32),
            pltpu.VMEM((members, half, unit), f32),
            pltpu.VMEM((members, half, unit), f32),
            dma((n,)),
            dma((n,)),
            dma((n_main, n_aux - 1)),
            dma((n_main, n_aux - 1)),
            dma((n_main,)),
            dma((n_main,)),
            dma((n_main, n_pts - 1)),
            dma((n_main, n_rep)),
            dma((n_tail, members - 1)),
            dma((n_tail, members - 1)),
            dma((n_tail, n_pts - 1)),
            dma((n_tail, members)),
        ],
        compiler_params=pltpu.CompilerParams(
            collective_id=1, has_side_effects=True, vmem_limit_bytes=24 << 20
        ),
    )(d, q, p, head)


def outer_kernel(scale, tile, slots, left, right, o_ref, buf, sem):
    steps = o_ref.shape[0] // tile

    def store(i):
        return pltpu.make_async_copy(
            buf.at[i % slots], o_ref.at[pl.ds(i * tile, tile)], sem.at[i % slots]
        )

    for i in range(steps):
        if i >= slots:
            store(i - slots).wait()
        buf[i % slots] = (
            lax.dot_general(
                left[:, i * tile : (i + 1) * tile], right[...],
                (((0,), (0,)), ((), ())), preferred_element_type=jnp.float32,
            )
            * scale
        )
        store(i).start()
    for i in range(max(0, steps - slots), steps):
        store(i).wait()


def outer(left, right, scale, tile=256, slots=4):
    n_rows, n_cols = left.shape[1], right.shape[1]
    tile = min(tile, n_rows)
    vmem = pl.BlockSpec(memory_space=pltpu.VMEM)
    return pl.pallas_call(
        functools.partial(outer_kernel, scale, tile, slots),
        in_specs=[vmem] * 2,
        out_specs=pl.BlockSpec(memory_space=pl.ANY),
        out_shape=jax.ShapeDtypeStruct((n_rows, n_cols), jnp.float32),
        scratch_shapes=[
            pltpu.VMEM((slots, tile, n_cols), jnp.float32),
            pltpu.SemaphoreType.DMA((slots,)),
        ],
        compiler_params=pltpu.CompilerParams(vmem_limit_bytes=20 << 20),
    )(left, right)


def per_device(density_slab, orbitals):
    left, right = factors(density_slab, orbitals)
    return outer(left, right, 1.0 / density_slab.shape[0])


def solution(mesh):
    return jax.shard_map(
        per_device,
        mesh=mesh,
        in_specs=(P("groups", "aux", "rep"), P(("groups", "rep"), "pts")),
        out_specs=P(("groups", "pts"), ("aux", "rep")),
        check_vma=False,
    )
```

```python
import functools

import jax
import jax.numpy as jnp
from jax import lax
from jax.experimental import pallas as pl
from jax.experimental.pallas import tpu as pltpu
from jax.sharding import PartitionSpec as P


MESH = pl.DeviceIdType.MESH
HEAD = 2


def split(w):
    high = w.astype(jnp.bfloat16)
    return high, (w - high.astype(jnp.float32)).astype(jnp.bfloat16)


def plan(own_pts, block):
    unit = max(128, block // 2)
    early = [(0, (HEAD + 1) * unit)]
    early += [(t, unit) for t in range((HEAD + 1) * unit, own_pts - 3 * unit, unit)]
    late = [(t, unit) for t in range(own_pts - 3 * unit, own_pts - unit, unit)]
    fine = unit // 2 if unit >= 256 else unit
    tail = [(t, fine) for t in range(own_pts - unit, own_pts, fine)]
    return unit, early, late, tail


def partial_weights(d_ref, q_ref, p_ref, out_ref, t, width, halfway=None):
    n_k, n_p, n_q = d_ref.shape
    group = max(1, 512 // n_p)
    there = slice(t, t + width)
    q_rows = q_ref[:, there]
    p_rows = p_ref[:, there].astype(jnp.float32)
    for k in range(0, n_k, group):
        if halfway is not None and k == n_k // 2:
            halfway()
        lhs = d_ref[k : k + group].reshape(group * n_p, n_q)
        c = jnp.dot(lhs, q_rows, preferred_element_type=jnp.float32)
        for j in range(group):
            term = c[j * n_p : (j + 1) * n_p] * p_rows
            out_ref[k + j : k + j + 1, there] = jnp.sum(term, axis=0, keepdims=True)


def arrived(ref, sem):
    pltpu.make_async_copy(ref, ref, sem).wait()


def load_kernel(
    unit, d_hbm, orb_hbm, d_ref, q_ref, p_ref, part_ref, d_sem, q_sem, p_sem, ps_sem
):
    n_k, n_p, n_q = d_hbm.shape
    own_pts = orb_hbm.shape[1]
    spans = [pl.ds(g * unit, unit) for g in range(HEAD)]
    spans.append(pl.ds(HEAD * unit, own_pts - HEAD * unit))
    a, r = lax.axis_index("aux"), lax.axis_index("rep")
    first = a * n_p
    owner, offset = first // n_q, pl.multiple_of(first % n_q, n_p)

    half = n_k // 2

    def d_copy(i):
        ks = pl.ds(((1 - r + i) % 2) * half, half)
        return pltpu.make_async_copy(
            d_hbm.at[ks], d_ref.at[pl.ds(i * half, half)], d_sem.at[i]
        )

    def q_copy(g):
        return pltpu.make_async_copy(
            orb_hbm.at[:, spans[g]], q_ref.at[:, spans[g]], q_sem.at[g]
        )

    def p_local(g):
        return pltpu.make_async_copy(
            orb_hbm.at[pl.ds(offset, n_p), spans[g]], p_ref.at[:, spans[g]], p_sem.at[g]
        )

    def p_remote(g):
        return pltpu.make_async_remote_copy(
            orb_hbm.at[pl.ds(offset, n_p), spans[g]], p_ref.at[:, spans[g]],
            ps_sem.at[g], p_sem.at[g],
            device_id={"rep": 1 - r}, device_id_type=MESH,
        )

    def send_p(g):
        @pl.when(owner == r)
        def _():
            p_remote(g).start()
            p_local(g).start()

    def p_wait(g):
        @pl.when(owner == r)
        def _():
            p_local(g).wait()

        @pl.when(owner != r)
        def _():
            p_remote(g).wait_recv()

    barrier = pltpu.get_barrier_semaphore()
    pl.semaphore_signal(barrier, inc=1, device_id={"rep": 1 - r}, device_id_type=MESH)
    q_copy(0).start()
    d_copy(0).start()
    pl.semaphore_wait(barrier, 1)
    send_p(0)
    q_copy(0).wait()
    d_copy(1).start()
    p_wait(0)
    d_copy(0).wait()
    q_copy(1).start()
    send_p(1)

    def second_half():
        d_copy(1).wait()
        for g in range(2, len(spans)):
            q_copy(g).start()
            send_p(g)

    for g in range(HEAD):
        if g > 0:
            q_copy(g).wait()
            p_wait(g)
        partial_weights(
            d_ref, q_ref, p_ref, part_ref, g * unit, unit,
            second_half if g == 0 else None,
        )
    for g in range(HEAD, len(spans)):
        q_copy(g).wait()
        p_wait(g)

    @pl.when(owner == r)
    def _():
        for g in range(len(spans)):
            p_remote(g).wait_send()


def share_kernel(
    sizes, early, late, tail, d_ref, q_ref, p_ref, head_ref, left_ref, right_ref,
    part, pair, rs_src, rs_dst, ag_buf, z_buf, tot, cols_buf, bc, xd,
    pair_send, pair_recv, rs_send, rs_recv, ag_send, ag_recv, z_send, z_recv,
    core_send, core_recv, x_send, x_recv, bc_send, bc_recv, xd_send, xd_recv,
):
    n_aux, n_pts, n_rep, block, unit = sizes
    n_k = d_ref.shape[0]
    half = n_k // n_rep
    rows = half // n_aux
    members = n_aux * n_rep
    blocks = members // n_pts
    a, x, r = lax.axis_index("aux"), lax.axis_index("pts"), lax.axis_index("rep")
    me = a * n_rep + r
    home = me // blocks
    mine = me % blocks
    every = early + late + tail
    n, n_early, n_main = len(every), len(early), len(early) + len(late)
    middle, begin = late[0][0], tail[0][0]
    edges = sorted({middle, begin} | {t for t, _ in late} | set(range(0, begin, block)))
    pieces = [(t, e - t) for t, e in zip(edges[:-1], edges[1:])]

    def member(j):
        return {"aux": j // n_rep, "rep": j % n_rep}

    def along(step):
        return {"aux": (a + step) % n_aux}

    def send(src, dst, send_sem, recv_sem, target):
        return pltpu.make_async_remote_copy(
            src, dst, send_sem, recv_sem, device_id=target, device_id_type=MESH
        )

    def span(c):
        return pl.ds(*every[c])

    def late_span(c):
        return pl.ds(every[c][0] - middle, every[c][1])

    def tail_span(c):
        return pl.ds(every[c][0] - begin, every[c][1])

    def pair_copy(c):
        return send(
            part.at[0:half, span(c)], pair.at[:, span(c)],
            pair_send.at[0], pair_recv.at[c], {"rep": 1 - r},
        )

    def x_owner(t):
        return x * blocks + t // block

    def x_target(t, step):
        return {**member(x_owner(t)), "pts": (x + step) % n_pts}

    def x_copy(i, step):
        t, width = pieces[i]
        return send(
            tot.at[r, :, pl.ds(t, width)], cols_buf.at[r, :, pl.ds(t % block, width)],
            x_send.at[i, step - 1], x_recv.at[0], x_target(t, step),
        )

    barrier = pltpu.get_barrier_semaphore()
    for step in range(1, members):
        pl.semaphore_signal(
            barrier, inc=1, device_id=member((me + step) % members), device_id_type=MESH
        )

    @pl.when(home != x)
    def _():
        for i in range(members):
            source = {"aux": i // n_rep, "rep": i % n_rep, "pts": home}
            pl.semaphore_signal(barrier, inc=1, device_id=source, device_id_type=MESH)

    part[:, 0 : HEAD * unit] = head_ref[...]

    def exchange(c):
        arrived(pair.at[:, span(c)], pair_recv.at[c])
        total = part[half:n_k, span(c)] + pair[:, span(c)]
        if c < n_early:
            for i in range(n_aux):
                rs_src[i, :, span(c)] = total[i * rows : (i + 1) * rows]
            for step in range(1, n_aux):
                send(
                    rs_src.at[(a + step) % n_aux, :, span(c)],
                    rs_dst.at[step - 1, :, span(c)],
                    rs_send.at[0], rs_recv.at[c], along(step),
                ).start()
        elif c < n_main:
            z_buf[a, :, late_span(c)] = total
            own = z_buf.at[a, :, late_span(c)]
            for step in range(1, n_aux):
                send(own, own, z_send.at[0], z_recv.at[c - n_early], along(step)).start()
        else:
            bc[me, :, tail_span(c)] = total
            own = bc.at[me, :, tail_span(c)]
            for step in range(1, members):
                send(
                    own, own, bc_send.at[0], bc_recv.at[c - n_main],
                    member((me + step) % members),
                ).start()
            for step in range(1, n_pts):
                send(
                    own, xd.at[me, :, tail_span(c)], xd_send.at[0], xd_recv.at[0],
                    x_target(every[c][0], step),
                ).start()

    def spread(c):
        arrived(rs_dst.at[:, :, span(c)], rs_recv.at[c])
        total = rs_src[a, :, span(c)]
        for step in range(1, n_aux):
            total = total + rs_dst[step - 1, :, span(c)]
        ag_buf[a, :, span(c)] = total
        own = ag_buf.at[a, :, span(c)]
        for step in range(1, n_aux):
            send(own, own, ag_send.at[0], ag_recv.at[c], along(step)).start()

    def pass_on(i, t, width):
        own = tot.at[r, :, pl.ds(t, width)]
        send(own, own, core_send.at[0], core_recv.at[i], {"rep": 1 - r}).start()
        for k, (start, _) in enumerate(pieces):
            if t <= start < t + width:

                @pl.when(x_owner(start) // n_rep == a)
                def _(k=k):
                    for step in range(1, n_pts):
                        x_copy(k, step).start()

    def finish_early():
        for c in range(n_early):
            arrived(rs_dst.at[:, :, span(c)], ag_recv.at[c])
            for i in range(n_aux):
                tot[r, pl.ds(i * rows, rows), span(c)] = ag_buf[i, :, span(c)]
        pass_on(0, 0, middle)

    def finish_late(c):
        arrived(z_buf.at[0 : n_aux - 1, :, late_span(c)], z_recv.at[c - n_early])
        total = z_buf[0, :, late_span(c)]
        for i in range(1, n_aux):
            total = total + z_buf[i, :, late_span(c)]
        tot[r, :, span(c)] = total
        pass_on(c - n_early + 1, *every[c])

    def place(t, width, w):
        there = pl.ds(t, width)
        high, low = split(w)
        left_ref[0:n_k, there] = high
        left_ref[n_k : 2 * n_k, there] = high
        left_ref[2 * n_k : 3 * n_k, there] = low

    def assemble(i, t, width):
        there = pl.ds(t, width)
        arrived(tot.at[0, :, there], core_recv.at[i])
        place(t, width, jnp.concatenate([tot[j, :, there] for j in range(n_rep)], axis=0))

    def gathered(ref, c):
        sums = []
        for i in range(n_rep):
            total = ref[i, :, tail_span(c)]
            for j in range(1, n_aux):
                total = total + ref[j * n_rep + i, :, tail_span(c)]
            sums.append(total)
        return sums

    def halfway(c):
        pair_copy(c).start()
        if c > n_main:
            exchange(c - 1)

    for c in range(n):
        t, width = every[c]
        start = max(t, HEAD * unit)
        partial_weights(
            d_ref, q_ref, p_ref, part, start, t + width - start,
            functools.partial(halfway, c) if c > 0 else None,
        )
        if c == 0:
            pl.semaphore_wait(barrier, members - 1 + (n_pts - 1) * blocks)
            pair_copy(0).start()
        for i in range(n_early):
            if c == max(i, 1) + 2:
                spread(i)
        if c == 1:
            exchange(0)
        if 0 < c < n_main or c == n - 1:
            exchange(c)

    finish_early()
    for c in range(n_early, n_main):
        finish_late(c)
    assemble(0, 0, middle)
    for c in range(n_early, n_main):
        assemble(c - n_early + 1, *every[c])

    for c in range(n_main, n):
        arrived(bc.at[0 : members - 1, :, tail_span(c)], bc_recv.at[c - n_main])
        sums = gathered(bc, c)
        for i in range(n_rep):
            tot[i, :, span(c)] = sums[i]
        place(*every[c], jnp.concatenate(sums, axis=0))

    @pl.when(home == x)
    def _():
        there = pl.ds(pl.multiple_of(mine * block, block), block)
        for i in range(n_rep):
            cols_buf[i] = tot[i, :, there]

    @pl.when((home != x) & (mine != blocks - 1))
    def _():
        arrived(cols_buf, x_recv.at[0])

    @pl.when((home != x) & (mine == blocks - 1))
    def _():
        arrived(cols_buf.at[:, :, 0 : begin % block], x_recv.at[0])
        arrived(xd, xd_recv.at[0])
        for c in range(n_main, n):
            for i, total in enumerate(gathered(xd, c)):
                cols_buf[i, :, pl.ds(every[c][0] % block, every[c][1])] = total

    high, low = split(jnp.concatenate([cols_buf[i] for i in range(n_rep)], axis=0))
    right_ref[0:n_k, :] = high
    right_ref[n_k : 2 * n_k, :] = low
    right_ref[2 * n_k : 3 * n_k, :] = high

    arrived(pair, pair_send.at[0])
    arrived(rs_dst, rs_send.at[0])
    arrived(rs_dst, ag_send.at[0])
    arrived(z_buf.at[0 : n_aux - 1], z_send.at[0])
    arrived(tot.at[0, :, 0:begin], core_send.at[0])
    arrived(bc.at[0 : members - 1], bc_send.at[0])
    arrived(xd.at[0 : n_pts - 1], xd_send.at[0])
    for k, (start, _) in enumerate(pieces):

        @pl.when(x_owner(start) // n_rep == a)
        def _(k=k):
            for step in range(1, n_pts):
                x_copy(k, step).wait_send()


def factors(density, orbitals):
    n_k, n_p, n_q = density.shape
    own_pts = orbitals.shape[1]
    n_aux, n_pts, n_rep = (lax.axis_size(name) for name in ("aux", "pts", "rep"))
    members = n_aux * n_rep
    block = own_pts * n_pts // members
    half = n_k // n_rep
    rows = half // n_aux
    unit, early, late, tail = plan(own_pts, block)
    n_early, n_late, n_tail = len(early), len(late), len(tail)
    n = n_early + n_late + n_tail
    early_w, late_w, tail_w = (sum(w for _, w in part) for part in (early, late, tail))
    dma = pltpu.SemaphoreType.DMA
    f32, bf16 = jnp.float32, jnp.bfloat16
    vmem = pl.BlockSpec(memory_space=pltpu.VMEM)
    d, q, p, head = pl.pallas_call(
        functools.partial(load_kernel, unit),
        in_specs=[pl.BlockSpec(memory_space=pl.ANY)] * 2,
        out_specs=[vmem] * 4,
        out_shape=[
            pltpu.VMEM((n_k, n_p, n_q), bf16),
            pltpu.VMEM((n_q, own_pts), bf16),
            pltpu.VMEM((n_p, own_pts), bf16),
            pltpu.VMEM((n_k, HEAD * unit), f32),
        ],
        scratch_shapes=[
            dma((2,)),
            dma((HEAD + 1,)),
            dma((HEAD + 1,)),
            dma((HEAD + 1,)),
        ],
        compiler_params=pltpu.CompilerParams(
            collective_id=0, has_side_effects=True, vmem_limit_bytes=51 << 20
        ),
    )(density, orbitals)
    return pl.pallas_call(
        functools.partial(share_kernel, (n_aux, n_pts, n_rep, block, unit), early, late, tail),
        in_specs=[vmem] * 4,
        out_specs=[vmem] * 2,
        out_shape=[
            pltpu.VMEM((3 * n_k, own_pts), bf16),
            pltpu.VMEM((3 * n_k, block), bf16),
        ],
        scratch_shapes=[
            pltpu.VMEM((n_k, own_pts), f32),
            pltpu.VMEM((half, own_pts), f32),
            pltpu.VMEM((n_aux, rows, early_w), f32),
            pltpu.VMEM((n_aux - 1, rows, early_w), f32),
            pltpu.VMEM((n_aux, rows, early_w), f32),
            pltpu.VMEM((n_aux, half, late_w), f32),
            pltpu.VMEM((n_rep, half, own_pts), f32),
            pltpu.VMEM((n_rep, half, block), f32),
            pltpu.VMEM((members, half, tail_w), f32),
            pltpu.VMEM((members, half, tail_w), f32),
            dma((1,)),
            dma((n,)),
            dma((1,)),
            dma((n_early,)),
            dma((1,)),
            dma((n_early,)),
            dma((1,)),
            dma((n_late,)),
            dma((1,)),
            dma((n_late + 1,)),
            dma((own_pts // block + n_late, n_pts - 1)),
            dma((1,)),
            dma((1,)),
            dma((n_tail,)),
            dma((1,)),
            dma((1,)),
        ],
        compiler_params=pltpu.CompilerParams(
            collective_id=1, has_side_effects=True, vmem_limit_bytes=24 << 20
        ),
    )(d, q, p, head)


def outer_kernel(scale, tile, slots, left, right, o_ref, buf, sem):
    steps = o_ref.shape[0] // tile

    def store(i):
        return pltpu.make_async_copy(
            buf.at[i % slots], o_ref.at[pl.ds(i * tile, tile)], sem.at[i % slots]
        )

    for i in range(steps):
        if i >= slots:
            store(i - slots).wait()
        buf[i % slots] = (
            lax.dot_general(
                left[:, i * tile : (i + 1) * tile], right[...],
                (((0,), (0,)), ((), ())), preferred_element_type=jnp.float32,
            )
            * scale
        )
        store(i).start()
    for i in range(max(0, steps - slots), steps):
        store(i).wait()


def outer(left, right, scale, tile=256, slots=4):
    n_rows, n_cols = left.shape[1], right.shape[1]
    tile = min(tile, n_rows)
    vmem = pl.BlockSpec(memory_space=pltpu.VMEM)
    return pl.pallas_call(
        functools.partial(outer_kernel, scale, tile, slots),
        in_specs=[vmem] * 2,
        out_specs=pl.BlockSpec(memory_space=pl.ANY),
        out_shape=jax.ShapeDtypeStruct((n_rows, n_cols), jnp.float32),
        scratch_shapes=[
            pltpu.VMEM((slots, tile, n_cols), jnp.float32),
            pltpu.SemaphoreType.DMA((slots,)),
        ],
        compiler_params=pltpu.CompilerParams(vmem_limit_bytes=20 << 20),
    )(left, right)


def per_device(density_slab, orbitals):
    left, right = factors(density_slab, orbitals)
    return outer(left, right, 1.0 / density_slab.shape[0])


def solution(mesh):
    return jax.shard_map(
        per_device,
        mesh=mesh,
        in_specs=(P("groups", "aux", "rep"), P(("groups", "rep"), "pts")),
        out_specs=P(("groups", "pts"), ("aux", "rep")),
        check_vma=False,
    )
```

```python
import functools

import jax
import jax.numpy as jnp
from jax import lax
from jax.experimental import pallas as pl
from jax.experimental.pallas import tpu as pltpu
from jax.sharding import PartitionSpec as P


MESH = pl.DeviceIdType.MESH
HEAD = 2


def split(w):
    high = w.astype(jnp.bfloat16)
    return high, (w - high.astype(jnp.float32)).astype(jnp.bfloat16)


def plan(own_pts, block):
    unit = max(128, block // 2)
    early = [(0, (HEAD + 1) * unit)]
    early += [(t, unit) for t in range((HEAD + 1) * unit, own_pts - 3 * unit, unit)]
    late = [(t, unit) for t in range(own_pts - 3 * unit, own_pts - unit, unit)]
    fine = unit // 2 if unit >= 256 else unit
    late += [(t, fine) for t in range(own_pts - unit, own_pts - fine, fine)]
    tail = [(own_pts - fine, fine)]
    return unit, early, late, tail


def partial_weights(d_ref, q_ref, p_ref, out_ref, t, width, halfway=None):
    n_k, n_p, n_q = d_ref.shape
    group = max(1, 512 // n_p)
    there = slice(t, t + width)
    q_rows = q_ref[:, there]
    p_rows = p_ref[:, there].astype(jnp.float32)
    for k in range(0, n_k, group):
        if halfway is not None and k == n_k // 2:
            halfway()
        lhs = d_ref[k : k + group].reshape(group * n_p, n_q)
        c = jnp.dot(lhs, q_rows, preferred_element_type=jnp.float32)
        for j in range(group):
            term = c[j * n_p : (j + 1) * n_p] * p_rows
            out_ref[k + j : k + j + 1, there] = jnp.sum(term, axis=0, keepdims=True)


def arrived(ref, sem):
    pltpu.make_async_copy(ref, ref, sem).wait()


def load_kernel(
    unit, d_hbm, orb_hbm, d_ref, q_ref, p_ref, part_ref, d_sem, q_sem, p_sem, ps_sem
):
    n_k, n_p, n_q = d_hbm.shape
    own_pts = orb_hbm.shape[1]
    spans = [pl.ds(g * unit, unit) for g in range(HEAD)]
    spans.append(pl.ds(HEAD * unit, own_pts - HEAD * unit))
    a, r = lax.axis_index("aux"), lax.axis_index("rep")
    first = a * n_p
    owner, offset = first // n_q, pl.multiple_of(first % n_q, n_p)

    half = n_k // 2

    def d_copy(i):
        ks = pl.ds(((1 - r + i) % 2) * half, half)
        return pltpu.make_async_copy(
            d_hbm.at[ks], d_ref.at[pl.ds(i * half, half)], d_sem.at[i]
        )

    def q_copy(g):
        return pltpu.make_async_copy(
            orb_hbm.at[:, spans[g]], q_ref.at[:, spans[g]], q_sem.at[g]
        )

    def p_local(g):
        return pltpu.make_async_copy(
            orb_hbm.at[pl.ds(offset, n_p), spans[g]], p_ref.at[:, spans[g]], p_sem.at[g]
        )

    def p_remote(g):
        return pltpu.make_async_remote_copy(
            orb_hbm.at[pl.ds(offset, n_p), spans[g]], p_ref.at[:, spans[g]],
            ps_sem.at[g], p_sem.at[g],
            device_id={"rep": 1 - r}, device_id_type=MESH,
        )

    def send_p(g):
        @pl.when(owner == r)
        def _():
            p_remote(g).start()
            p_local(g).start()

    def p_wait(g):
        @pl.when(owner == r)
        def _():
            p_local(g).wait()

        @pl.when(owner != r)
        def _():
            p_remote(g).wait_recv()

    barrier = pltpu.get_barrier_semaphore()
    pl.semaphore_signal(barrier, inc=1, device_id={"rep": 1 - r}, device_id_type=MESH)
    q_copy(0).start()
    d_copy(0).start()
    pl.semaphore_wait(barrier, 1)
    send_p(0)
    q_copy(0).wait()
    d_copy(1).start()
    p_wait(0)
    d_copy(0).wait()
    q_copy(1).start()
    send_p(1)

    def second_half():
        d_copy(1).wait()
        for g in range(2, len(spans)):
            q_copy(g).start()
            send_p(g)

    for g in range(HEAD):
        if g > 0:
            q_copy(g).wait()
            p_wait(g)
        partial_weights(
            d_ref, q_ref, p_ref, part_ref, g * unit, unit,
            second_half if g == 0 else None,
        )
    for g in range(HEAD, len(spans)):
        q_copy(g).wait()
        p_wait(g)

    @pl.when(owner == r)
    def _():
        for g in range(len(spans)):
            p_remote(g).wait_send()


def share_kernel(
    sizes, early, late, tail, d_ref, q_ref, p_ref, head_ref, left_ref, right_ref,
    part, pair, rs_src, rs_dst, ag_buf, z_buf, tot, cols_buf, bc, xd,
    pair_send, pair_recv, rs_send, rs_recv, ag_send, ag_recv, z_send, z_recv,
    core_send, core_recv, x_send, x_recv, bc_send, bc_recv, xd_send, xd_recv,
):
    n_aux, n_pts, n_rep, block, unit = sizes
    n_k = d_ref.shape[0]
    half = n_k // n_rep
    rows = half // n_aux
    members = n_aux * n_rep
    blocks = members // n_pts
    a, x, r = lax.axis_index("aux"), lax.axis_index("pts"), lax.axis_index("rep")
    me = a * n_rep + r
    home = me // blocks
    mine = me % blocks
    every = early + late + tail
    n, n_early, n_main = len(every), len(early), len(early) + len(late)
    middle, begin = late[0][0], tail[0][0]
    edges = sorted({middle, begin} | {t for t, _ in late} | set(range(0, begin, block)))
    pieces = [(t, e - t) for t, e in zip(edges[:-1], edges[1:])]

    def member(j):
        return {"aux": j // n_rep, "rep": j % n_rep}

    def along(step):
        return {"aux": (a + step) % n_aux}

    def send(src, dst, send_sem, recv_sem, target):
        return pltpu.make_async_remote_copy(
            src, dst, send_sem, recv_sem, device_id=target, device_id_type=MESH
        )

    def span(c):
        return pl.ds(*every[c])

    def late_span(c):
        return pl.ds(every[c][0] - middle, every[c][1])

    def tail_span(c):
        return pl.ds(every[c][0] - begin, every[c][1])

    def pair_copy(c):
        return send(
            part.at[0:half, span(c)], pair.at[:, span(c)],
            pair_send.at[0], pair_recv.at[c], {"rep": 1 - r},
        )

    def x_owner(t):
        return x * blocks + t // block

    def x_target(t, step):
        return {**member(x_owner(t)), "pts": (x + step) % n_pts}

    def x_copy(i, step):
        t, width = pieces[i]
        return send(
            tot.at[r, :, pl.ds(t, width)], cols_buf.at[r, :, pl.ds(t % block, width)],
            x_send.at[i, step - 1], x_recv.at[0], x_target(t, step),
        )

    barrier = pltpu.get_barrier_semaphore()
    for step in range(1, members):
        pl.semaphore_signal(
            barrier, inc=1, device_id=member((me + step) % members), device_id_type=MESH
        )

    @pl.when(home != x)
    def _():
        for i in range(members):
            source = {"aux": i // n_rep, "rep": i % n_rep, "pts": home}
            pl.semaphore_signal(barrier, inc=1, device_id=source, device_id_type=MESH)

    part[:, 0 : HEAD * unit] = head_ref[...]

    def exchange(c):
        arrived(pair.at[:, span(c)], pair_recv.at[c])
        total = part[half:n_k, span(c)] + pair[:, span(c)]
        if c < n_early:
            for i in range(n_aux):
                rs_src[i, :, span(c)] = total[i * rows : (i + 1) * rows]
            for step in range(1, n_aux):
                send(
                    rs_src.at[(a + step) % n_aux, :, span(c)],
                    rs_dst.at[step - 1, :, span(c)],
                    rs_send.at[0], rs_recv.at[c], along(step),
                ).start()
        elif c < n_main:
            z_buf[a, :, late_span(c)] = total
            own = z_buf.at[a, :, late_span(c)]
            for step in range(1, n_aux):
                send(own, own, z_send.at[0], z_recv.at[c - n_early], along(step)).start()
        else:
            bc[me, :, tail_span(c)] = total
            own = bc.at[me, :, tail_span(c)]
            for step in range(1, members):
                send(
                    own, own, bc_send.at[0], bc_recv.at[c - n_main],
                    member((me + step) % members),
                ).start()
            for step in range(1, n_pts):
                send(
                    own, xd.at[me, :, tail_span(c)], xd_send.at[0], xd_recv.at[0],
                    x_target(every[c][0], step),
                ).start()

    def spread(c):
        arrived(rs_dst.at[:, :, span(c)], rs_recv.at[c])
        total = rs_src[a, :, span(c)]
        for step in range(1, n_aux):
            total = total + rs_dst[step - 1, :, span(c)]
        ag_buf[a, :, span(c)] = total
        own = ag_buf.at[a, :, span(c)]
        for step in range(1, n_aux):
            send(own, own, ag_send.at[0], ag_recv.at[c], along(step)).start()

    def pass_on(i, t, width):
        own = tot.at[r, :, pl.ds(t, width)]
        send(own, own, core_send.at[0], core_recv.at[i], {"rep": 1 - r}).start()
        for k, (start, _) in enumerate(pieces):
            if t <= start < t + width:

                @pl.when(x_owner(start) // n_rep == a)
                def _(k=k):
                    for step in range(1, n_pts):
                        x_copy(k, step).start()

    def finish_early():
        for c in range(n_early):
            arrived(rs_dst.at[:, :, span(c)], ag_recv.at[c])
            for i in range(n_aux):
                tot[r, pl.ds(i * rows, rows), span(c)] = ag_buf[i, :, span(c)]
        pass_on(0, 0, middle)

    def finish_late(c):
        arrived(z_buf.at[0 : n_aux - 1, :, late_span(c)], z_recv.at[c - n_early])
        total = z_buf[0, :, late_span(c)]
        for i in range(1, n_aux):
            total = total + z_buf[i, :, late_span(c)]
        tot[r, :, span(c)] = total
        pass_on(c - n_early + 1, *every[c])

    def place(t, width, w):
        there = pl.ds(t, width)
        high, low = split(w)
        left_ref[0:n_k, there] = high
        left_ref[n_k : 2 * n_k, there] = high
        left_ref[2 * n_k : 3 * n_k, there] = low

    def assemble(i, t, width):
        there = pl.ds(t, width)
        arrived(tot.at[0, :, there], core_recv.at[i])
        place(t, width, jnp.concatenate([tot[j, :, there] for j in range(n_rep)], axis=0))

    def gathered(ref, c):
        sums = []
        for i in range(n_rep):
            total = ref[i, :, tail_span(c)]
            for j in range(1, n_aux):
                total = total + ref[j * n_rep + i, :, tail_span(c)]
            sums.append(total)
        return sums

    def halfway(c):
        pair_copy(c).start()
        if c == n - 1:
            exchange(c - 1)

    for c in range(n):
        t, width = every[c]
        start = max(t, HEAD * unit)
        partial_weights(
            d_ref, q_ref, p_ref, part, start, t + width - start,
            functools.partial(halfway, c) if c > 1 else None,
        )
        if c == 0:
            pl.semaphore_wait(barrier, members - 1 + (n_pts - 1) * blocks)
            pair_copy(0).start()
        if c == 1:
            pair_copy(1).start()
        for i in range(n_early):
            if c == (3 if i == 0 else 4):
                spread(i)
        if c == 1:
            exchange(0)
        if c == 2:
            exchange(1)
        if 1 < c < n - 2 or c == n - 1:
            exchange(c)

    finish_early()
    for c in range(n_early, n_main):
        finish_late(c)
    assemble(0, 0, middle)
    for c in range(n_early, n_main):
        assemble(c - n_early + 1, *every[c])

    for c in range(n_main, n):
        arrived(bc.at[0 : members - 1, :, tail_span(c)], bc_recv.at[c - n_main])
        sums = gathered(bc, c)
        for i in range(n_rep):
            tot[i, :, span(c)] = sums[i]
        place(*every[c], jnp.concatenate(sums, axis=0))

    @pl.when(home == x)
    def _():
        there = pl.ds(pl.multiple_of(mine * block, block), block)
        for i in range(n_rep):
            cols_buf[i] = tot[i, :, there]

    @pl.when((home != x) & (mine != blocks - 1))
    def _():
        arrived(cols_buf, x_recv.at[0])

    @pl.when((home != x) & (mine == blocks - 1))
    def _():
        arrived(cols_buf.at[:, :, 0 : begin % block], x_recv.at[0])
        arrived(xd, xd_recv.at[0])
        for c in range(n_main, n):
            for i, total in enumerate(gathered(xd, c)):
                cols_buf[i, :, pl.ds(every[c][0] % block, every[c][1])] = total

    high, low = split(jnp.concatenate([cols_buf[i] for i in range(n_rep)], axis=0))
    right_ref[0:n_k, :] = high
    right_ref[n_k : 2 * n_k, :] = low
    right_ref[2 * n_k : 3 * n_k, :] = high

    arrived(pair, pair_send.at[0])
    arrived(rs_dst, rs_send.at[0])
    arrived(rs_dst, ag_send.at[0])
    arrived(z_buf.at[0 : n_aux - 1], z_send.at[0])
    arrived(tot.at[0, :, 0:begin], core_send.at[0])
    arrived(bc.at[0 : members - 1], bc_send.at[0])
    arrived(xd.at[0 : n_pts - 1], xd_send.at[0])
    for k, (start, _) in enumerate(pieces):

        @pl.when(x_owner(start) // n_rep == a)
        def _(k=k):
            for step in range(1, n_pts):
                x_copy(k, step).wait_send()


def factors(density, orbitals):
    n_k, n_p, n_q = density.shape
    own_pts = orbitals.shape[1]
    n_aux, n_pts, n_rep = (lax.axis_size(name) for name in ("aux", "pts", "rep"))
    members = n_aux * n_rep
    block = own_pts * n_pts // members
    half = n_k // n_rep
    rows = half // n_aux
    unit, early, late, tail = plan(own_pts, block)
    n_early, n_late, n_tail = len(early), len(late), len(tail)
    n = n_early + n_late + n_tail
    early_w, late_w, tail_w = (sum(w for _, w in part) for part in (early, late, tail))
    dma = pltpu.SemaphoreType.DMA
    f32, bf16 = jnp.float32, jnp.bfloat16
    vmem = pl.BlockSpec(memory_space=pltpu.VMEM)
    d, q, p, head = pl.pallas_call(
        functools.partial(load_kernel, unit),
        in_specs=[pl.BlockSpec(memory_space=pl.ANY)] * 2,
        out_specs=[vmem] * 4,
        out_shape=[
            pltpu.VMEM((n_k, n_p, n_q), bf16),
            pltpu.VMEM((n_q, own_pts), bf16),
            pltpu.VMEM((n_p, own_pts), bf16),
            pltpu.VMEM((n_k, HEAD * unit), f32),
        ],
        scratch_shapes=[
            dma((2,)),
            dma((HEAD + 1,)),
            dma((HEAD + 1,)),
            dma((HEAD + 1,)),
        ],
        compiler_params=pltpu.CompilerParams(
            collective_id=0, has_side_effects=True, vmem_limit_bytes=51 << 20
        ),
    )(density, orbitals)
    return pl.pallas_call(
        functools.partial(share_kernel, (n_aux, n_pts, n_rep, block, unit), early, late, tail),
        in_specs=[vmem] * 4,
        out_specs=[vmem] * 2,
        out_shape=[
            pltpu.VMEM((3 * n_k, own_pts), bf16),
            pltpu.VMEM((3 * n_k, block), bf16),
        ],
        scratch_shapes=[
            pltpu.VMEM((n_k, own_pts), f32),
            pltpu.VMEM((half, own_pts), f32),
            pltpu.VMEM((n_aux, rows, early_w), f32),
            pltpu.VMEM((n_aux - 1, rows, early_w), f32),
            pltpu.VMEM((n_aux, rows, early_w), f32),
            pltpu.VMEM((n_aux, half, late_w), f32),
            pltpu.VMEM((n_rep, half, own_pts), f32),
            pltpu.VMEM((n_rep, half, block), f32),
            pltpu.VMEM((members, half, tail_w), f32),
            pltpu.VMEM((members, half, tail_w), f32),
            dma((1,)),
            dma((n,)),
            dma((1,)),
            dma((n_early,)),
            dma((1,)),
            dma((n_early,)),
            dma((1,)),
            dma((n_late,)),
            dma((1,)),
            dma((n_late + 1,)),
            dma((own_pts // block + n_late, n_pts - 1)),
            dma((1,)),
            dma((1,)),
            dma((n_tail,)),
            dma((1,)),
            dma((1,)),
        ],
        compiler_params=pltpu.CompilerParams(
            collective_id=1, has_side_effects=True, vmem_limit_bytes=24 << 20
        ),
    )(d, q, p, head)


def outer_kernel(scale, tile, slots, left, right, o_ref, buf, sem):
    steps = o_ref.shape[0] // tile

    def store(i):
        return pltpu.make_async_copy(
            buf.at[i % slots], o_ref.at[pl.ds(i * tile, tile)], sem.at[i % slots]
        )

    for i in range(steps):
        if i >= slots:
            store(i - slots).wait()
        buf[i % slots] = (
            lax.dot_general(
                left[:, i * tile : (i + 1) * tile], right[...],
                (((0,), (0,)), ((), ())), preferred_element_type=jnp.float32,
            )
            * scale
        )
        store(i).start()
    for i in range(max(0, steps - slots), steps):
        store(i).wait()


def outer(left, right, scale, tile=256, slots=4):
    n_rows, n_cols = left.shape[1], right.shape[1]
    tile = min(tile, n_rows)
    vmem = pl.BlockSpec(memory_space=pltpu.VMEM)
    return pl.pallas_call(
        functools.partial(outer_kernel, scale, tile, slots),
        in_specs=[vmem] * 2,
        out_specs=pl.BlockSpec(memory_space=pl.ANY),
        out_shape=jax.ShapeDtypeStruct((n_rows, n_cols), jnp.float32),
        scratch_shapes=[
            pltpu.VMEM((slots, tile, n_cols), jnp.float32),
            pltpu.SemaphoreType.DMA((slots,)),
        ],
        compiler_params=pltpu.CompilerParams(vmem_limit_bytes=20 << 20),
    )(left, right)


def per_device(density_slab, orbitals):
    left, right = factors(density_slab, orbitals)
    return outer(left, right, 1.0 / density_slab.shape[0])


def solution(mesh):
    return jax.shard_map(
        per_device,
        mesh=mesh,
        in_specs=(P("groups", "aux", "rep"), P(("groups", "rep"), "pts")),
        out_specs=P(("groups", "pts"), ("aux", "rep")),
        check_vma=False,
    )
```

```python
import functools

import jax
import jax.numpy as jnp
from jax import lax
from jax.experimental import pallas as pl
from jax.experimental.pallas import tpu as pltpu
from jax.sharding import PartitionSpec as P


MESH = pl.DeviceIdType.MESH
HEAD = 2


def split(w):
    high = w.astype(jnp.bfloat16)
    return high, (w - high.astype(jnp.float32)).astype(jnp.bfloat16)


def plan(own_pts, block):
    unit = max(128, block // 2)
    early = [(0, (HEAD + 1) * unit)]
    early += [(t, unit) for t in range((HEAD + 1) * unit, own_pts - 3 * unit, unit)]
    late = [(t, unit) for t in range(own_pts - 3 * unit, own_pts - unit, unit)]
    fine = unit // 2 if unit >= 256 else unit
    late += [(t, fine) for t in range(own_pts - unit, own_pts - fine, fine)]
    tail = [(own_pts - fine, fine)]
    return unit, early, late, tail


def partial_weights(d_ref, q_ref, p_ref, out_ref, t, width, halfway=None):
    n_k, n_p, n_q = d_ref.shape
    group = max(1, 512 // n_p)
    there = slice(t, t + width)
    q_rows = q_ref[:, there]
    p_rows = p_ref[:, there].astype(jnp.float32)
    for k in range(0, n_k, group):
        if halfway is not None and k == n_k // 2:
            halfway()
        lhs = d_ref[k : k + group].reshape(group * n_p, n_q)
        c = jnp.dot(lhs, q_rows, preferred_element_type=jnp.float32)
        for j in range(group):
            term = c[j * n_p : (j + 1) * n_p] * p_rows
            out_ref[k + j : k + j + 1, there] = jnp.sum(term, axis=0, keepdims=True)


def arrived(ref, sem):
    pltpu.make_async_copy(ref, ref, sem).wait()


def load_kernel(
    unit, d_hbm, orb_hbm, d_ref, q_ref, p_ref, part_ref, d_sem, q_sem, p_sem, ps_sem
):
    n_k, n_p, n_q = d_hbm.shape
    own_pts = orb_hbm.shape[1]
    spans = [pl.ds(g * unit, unit) for g in range(HEAD)]
    spans.append(pl.ds(HEAD * unit, own_pts - HEAD * unit))
    a, r = lax.axis_index("aux"), lax.axis_index("rep")
    first = a * n_p
    owner, offset = first // n_q, pl.multiple_of(first % n_q, n_p)

    half = n_k // 2

    def d_copy(i):
        ks = pl.ds(((1 - r + i) % 2) * half, half)
        return pltpu.make_async_copy(
            d_hbm.at[ks], d_ref.at[pl.ds(i * half, half)], d_sem.at[i]
        )

    def q_copy(g):
        return pltpu.make_async_copy(
            orb_hbm.at[:, spans[g]], q_ref.at[:, spans[g]], q_sem.at[g]
        )

    def p_local(g):
        return pltpu.make_async_copy(
            orb_hbm.at[pl.ds(offset, n_p), spans[g]], p_ref.at[:, spans[g]], p_sem.at[g]
        )

    def p_remote(g):
        return pltpu.make_async_remote_copy(
            orb_hbm.at[pl.ds(offset, n_p), spans[g]], p_ref.at[:, spans[g]],
            ps_sem.at[g], p_sem.at[g],
            device_id={"rep": 1 - r}, device_id_type=MESH,
        )

    def send_p(g):
        @pl.when(owner == r)
        def _():
            p_remote(g).start()
            p_local(g).start()

    def p_wait(g):
        @pl.when(owner == r)
        def _():
            p_local(g).wait()

        @pl.when(owner != r)
        def _():
            p_remote(g).wait_recv()

    barrier = pltpu.get_barrier_semaphore()
    pl.semaphore_signal(barrier, inc=1, device_id={"rep": 1 - r}, device_id_type=MESH)
    q_copy(0).start()
    d_copy(0).start()
    pl.semaphore_wait(barrier, 1)
    send_p(0)
    q_copy(0).wait()
    d_copy(1).start()
    p_wait(0)
    d_copy(0).wait()
    q_copy(1).start()
    send_p(1)

    def second_half():
        d_copy(1).wait()
        for g in range(2, len(spans)):
            q_copy(g).start()
            send_p(g)
        for g in range(1, HEAD):
            q_copy(g).wait()
            p_wait(g)

    for g in range(HEAD):
        partial_weights(
            d_ref, q_ref, p_ref, part_ref, g * unit, unit,
            second_half if g == 0 else None,
        )
    for g in range(HEAD, len(spans)):
        q_copy(g).wait()
        p_wait(g)

    @pl.when(owner == r)
    def _():
        for g in range(len(spans)):
            p_remote(g).wait_send()


def share_kernel(
    sizes, early, late, tail, d_ref, q_ref, p_ref, head_ref, left_ref, right_ref,
    part, pair, rs_src, rs_dst, ag_buf, z_buf, tot, cols_buf, bc, xd,
    pair_send, pair_recv, rs_send, rs_recv, ag_send, ag_recv, z_send, z_recv,
    core_send, core_recv, x_send, x_recv, bc_send, bc_recv, xd_send, xd_recv,
):
    n_aux, n_pts, n_rep, block, unit = sizes
    n_k = d_ref.shape[0]
    half = n_k // n_rep
    rows = half // n_aux
    members = n_aux * n_rep
    blocks = members // n_pts
    a, x, r = lax.axis_index("aux"), lax.axis_index("pts"), lax.axis_index("rep")
    me = a * n_rep + r
    home = me // blocks
    mine = me % blocks
    every = early + late + tail
    n, n_early, n_main = len(every), len(early), len(early) + len(late)
    middle, begin = late[0][0], tail[0][0]
    edges = sorted({middle, begin} | {t for t, _ in late} | set(range(0, begin, block)))
    pieces = [(t, e - t) for t, e in zip(edges[:-1], edges[1:])]

    def member(j):
        return {"aux": j // n_rep, "rep": j % n_rep}

    def along(step):
        return {"aux": (a + step) % n_aux}

    def send(src, dst, send_sem, recv_sem, target):
        return pltpu.make_async_remote_copy(
            src, dst, send_sem, recv_sem, device_id=target, device_id_type=MESH
        )

    def span(c):
        return pl.ds(*every[c])

    def late_span(c):
        return pl.ds(every[c][0] - middle, every[c][1])

    def tail_span(c):
        return pl.ds(every[c][0] - begin, every[c][1])

    def pair_copy(c):
        return send(
            part.at[0:half, span(c)], pair.at[:, span(c)],
            pair_send.at[0], pair_recv.at[c], {"rep": 1 - r},
        )

    def x_owner(t):
        return x * blocks + t // block

    def x_target(t, step):
        return {**member(x_owner(t)), "pts": (x + step) % n_pts}

    def x_copy(i, step):
        t, width = pieces[i]
        return send(
            tot.at[r, :, pl.ds(t, width)], cols_buf.at[r, :, pl.ds(t % block, width)],
            x_send.at[i, step - 1], x_recv.at[0], x_target(t, step),
        )

    barrier = pltpu.get_barrier_semaphore()
    for step in range(1, members):
        pl.semaphore_signal(
            barrier, inc=1, device_id=member((me + step) % members), device_id_type=MESH
        )

    @pl.when(home != x)
    def _():
        for i in range(members):
            source = {"aux": i // n_rep, "rep": i % n_rep, "pts": home}
            pl.semaphore_signal(barrier, inc=1, device_id=source, device_id_type=MESH)

    part[:, 0 : HEAD * unit] = head_ref[...]

    def exchange(c):
        arrived(pair.at[:, span(c)], pair_recv.at[c])
        total = part[half:n_k, span(c)] + pair[:, span(c)]
        if c < n_early:
            for i in range(n_aux):
                rs_src[i, :, span(c)] = total[i * rows : (i + 1) * rows]
            for step in range(1, n_aux):
                send(
                    rs_src.at[(a + step) % n_aux, :, span(c)],
                    rs_dst.at[step - 1, :, span(c)],
                    rs_send.at[0], rs_recv.at[c], along(step),
                ).start()
        elif c < n_main:
            z_buf[a, :, late_span(c)] = total
            own = z_buf.at[a, :, late_span(c)]
            for step in range(1, n_aux):
                send(own, own, z_send.at[0], z_recv.at[c - n_early], along(step)).start()
        else:
            bc[me, :, tail_span(c)] = total
            own = bc.at[me, :, tail_span(c)]
            for step in range(1, members):
                send(
                    own, own, bc_send.at[0], bc_recv.at[c - n_main],
                    member((me + step) % members),
                ).start()
            for step in range(1, n_pts):
                send(
                    own, xd.at[me, :, tail_span(c)], xd_send.at[0], xd_recv.at[0],
                    x_target(every[c][0], step),
                ).start()

    def spread(c):
        arrived(rs_dst.at[:, :, span(c)], rs_recv.at[c])
        total = rs_src[a, :, span(c)]
        for step in range(1, n_aux):
            total = total + rs_dst[step - 1, :, span(c)]
        ag_buf[a, :, span(c)] = total
        own = ag_buf.at[a, :, span(c)]
        for step in range(1, n_aux):
            send(own, own, ag_send.at[0], ag_recv.at[c], along(step)).start()

    def pass_on(i, t, width):
        own = tot.at[r, :, pl.ds(t, width)]
        send(own, own, core_send.at[0], core_recv.at[i], {"rep": 1 - r}).start()
        for k, (start, _) in enumerate(pieces):
            if t <= start < t + width:

                @pl.when(x_owner(start) // n_rep == a)
                def _(k=k):
                    for step in range(1, n_pts):
                        x_copy(k, step).start()

    def finish_early():
        for c in range(n_early):
            arrived(rs_dst.at[:, :, span(c)], ag_recv.at[c])
            for i in range(n_aux):
                tot[r, pl.ds(i * rows, rows), span(c)] = ag_buf[i, :, span(c)]
        pass_on(0, 0, middle)

    def finish_late(c):
        arrived(z_buf.at[0 : n_aux - 1, :, late_span(c)], z_recv.at[c - n_early])
        total = z_buf[0, :, late_span(c)]
        for i in range(1, n_aux):
            total = total + z_buf[i, :, late_span(c)]
        tot[r, :, span(c)] = total
        pass_on(c - n_early + 1, *every[c])

    def place(t, width, w):
        there = pl.ds(t, width)
        high, low = split(w)
        left_ref[0:n_k, there] = high
        left_ref[n_k : 2 * n_k, there] = high
        left_ref[2 * n_k : 3 * n_k, there] = low

    def assemble(i, t, width):
        there = pl.ds(t, width)
        arrived(tot.at[0, :, there], core_recv.at[i])
        place(t, width, jnp.concatenate([tot[j, :, there] for j in range(n_rep)], axis=0))

    def gathered(ref, c):
        sums = []
        for i in range(n_rep):
            total = ref[i, :, tail_span(c)]
            for j in range(1, n_aux):
                total = total + ref[j * n_rep + i, :, tail_span(c)]
            sums.append(total)
        return sums

    def halfway(c):
        pair_copy(c).start()
        if c in (n_early + 1, n - 1):
            exchange(c - 1)

    for c in range(n):
        t, width = every[c]
        start = max(t, HEAD * unit)
        partial_weights(
            d_ref, q_ref, p_ref, part, start, t + width - start,
            functools.partial(halfway, c) if c > 1 and c != n_early else None,
        )
        if c == 0:
            pl.semaphore_wait(barrier, members - 1 + (n_pts - 1) * blocks)
            pair_copy(0).start()
        if c in (1, n_early):
            pair_copy(c).start()
        for i in range(n_early):
            if c == (3 if i == 0 else 4):
                spread(i)
        if c == 1:
            exchange(0)
        if c == 2:
            exchange(1)
        if 1 < c < n - 2 and c != n_early or c == n - 1:
            exchange(c)

    finish_early()
    for c in range(n_early, n_main):
        finish_late(c)
    assemble(0, 0, middle)
    for c in range(n_early, n_main):
        assemble(c - n_early + 1, *every[c])

    for c in range(n_main, n):
        arrived(bc.at[0 : members - 1, :, tail_span(c)], bc_recv.at[c - n_main])
        sums = gathered(bc, c)
        for i in range(n_rep):
            tot[i, :, span(c)] = sums[i]
        place(*every[c], jnp.concatenate(sums, axis=0))

    @pl.when(home == x)
    def _():
        there = pl.ds(pl.multiple_of(mine * block, block), block)
        for i in range(n_rep):
            cols_buf[i] = tot[i, :, there]

    @pl.when((home != x) & (mine != blocks - 1))
    def _():
        arrived(cols_buf, x_recv.at[0])

    @pl.when((home != x) & (mine == blocks - 1))
    def _():
        arrived(cols_buf.at[:, :, 0 : begin % block], x_recv.at[0])
        arrived(xd, xd_recv.at[0])
        for c in range(n_main, n):
            for i, total in enumerate(gathered(xd, c)):
                cols_buf[i, :, pl.ds(every[c][0] % block, every[c][1])] = total

    high, low = split(jnp.concatenate([cols_buf[i] for i in range(n_rep)], axis=0))
    right_ref[0:n_k, :] = high
    right_ref[n_k : 2 * n_k, :] = low
    right_ref[2 * n_k : 3 * n_k, :] = high

    arrived(pair, pair_send.at[0])
    arrived(rs_dst, rs_send.at[0])
    arrived(rs_dst, ag_send.at[0])
    arrived(z_buf.at[0 : n_aux - 1], z_send.at[0])
    arrived(tot.at[0, :, 0:begin], core_send.at[0])
    arrived(bc.at[0 : members - 1], bc_send.at[0])
    arrived(xd.at[0 : n_pts - 1], xd_send.at[0])
    for k, (start, _) in enumerate(pieces):

        @pl.when(x_owner(start) // n_rep == a)
        def _(k=k):
            for step in range(1, n_pts):
                x_copy(k, step).wait_send()


def factors(density, orbitals):
    n_k, n_p, n_q = density.shape
    own_pts = orbitals.shape[1]
    n_aux, n_pts, n_rep = (lax.axis_size(name) for name in ("aux", "pts", "rep"))
    members = n_aux * n_rep
    block = own_pts * n_pts // members
    half = n_k // n_rep
    rows = half // n_aux
    unit, early, late, tail = plan(own_pts, block)
    n_early, n_late, n_tail = len(early), len(late), len(tail)
    n = n_early + n_late + n_tail
    early_w, late_w, tail_w = (sum(w for _, w in part) for part in (early, late, tail))
    dma = pltpu.SemaphoreType.DMA
    f32, bf16 = jnp.float32, jnp.bfloat16
    vmem = pl.BlockSpec(memory_space=pltpu.VMEM)
    d, q, p, head = pl.pallas_call(
        functools.partial(load_kernel, unit),
        in_specs=[pl.BlockSpec(memory_space=pl.ANY)] * 2,
        out_specs=[vmem] * 4,
        out_shape=[
            pltpu.VMEM((n_k, n_p, n_q), bf16),
            pltpu.VMEM((n_q, own_pts), bf16),
            pltpu.VMEM((n_p, own_pts), bf16),
            pltpu.VMEM((n_k, HEAD * unit), f32),
        ],
        scratch_shapes=[
            dma((2,)),
            dma((HEAD + 1,)),
            dma((HEAD + 1,)),
            dma((HEAD + 1,)),
        ],
        compiler_params=pltpu.CompilerParams(
            collective_id=0, has_side_effects=True, vmem_limit_bytes=51 << 20
        ),
    )(density, orbitals)
    return pl.pallas_call(
        functools.partial(share_kernel, (n_aux, n_pts, n_rep, block, unit), early, late, tail),
        in_specs=[vmem] * 4,
        out_specs=[vmem] * 2,
        out_shape=[
            pltpu.VMEM((3 * n_k, own_pts), bf16),
            pltpu.VMEM((3 * n_k, block), bf16),
        ],
        scratch_shapes=[
            pltpu.VMEM((n_k, own_pts), f32),
            pltpu.VMEM((half, own_pts), f32),
            pltpu.VMEM((n_aux, rows, early_w), f32),
            pltpu.VMEM((n_aux - 1, rows, early_w), f32),
            pltpu.VMEM((n_aux, rows, early_w), f32),
            pltpu.VMEM((n_aux, half, late_w), f32),
            pltpu.VMEM((n_rep, half, own_pts), f32),
            pltpu.VMEM((n_rep, half, block), f32),
            pltpu.VMEM((members, half, tail_w), f32),
            pltpu.VMEM((members, half, tail_w), f32),
            dma((1,)),
            dma((n,)),
            dma((1,)),
            dma((n_early,)),
            dma((1,)),
            dma((n_early,)),
            dma((1,)),
            dma((n_late,)),
            dma((1,)),
            dma((n_late + 1,)),
            dma((own_pts // block + n_late, n_pts - 1)),
            dma((1,)),
            dma((1,)),
            dma((n_tail,)),
            dma((1,)),
            dma((1,)),
        ],
        compiler_params=pltpu.CompilerParams(
            collective_id=1, has_side_effects=True, vmem_limit_bytes=24 << 20
        ),
    )(d, q, p, head)


def outer_kernel(scale, tile, slots, left, right, o_ref, buf, sem):
    steps = o_ref.shape[0] // tile

    def store(i):
        return pltpu.make_async_copy(
            buf.at[i % slots], o_ref.at[pl.ds(i * tile, tile)], sem.at[i % slots]
        )

    for i in range(steps):
        if i >= slots:
            store(i - slots).wait()
        buf[i % slots] = (
            lax.dot_general(
                left[:, i * tile : (i + 1) * tile], right[...],
                (((0,), (0,)), ((), ())), preferred_element_type=jnp.float32,
            )
            * scale
        )
        store(i).start()
    for i in range(max(0, steps - slots), steps):
        store(i).wait()


def outer(left, right, scale, tile=256, slots=4):
    n_rows, n_cols = left.shape[1], right.shape[1]
    tile = min(tile, n_rows)
    vmem = pl.BlockSpec(memory_space=pltpu.VMEM)
    return pl.pallas_call(
        functools.partial(outer_kernel, scale, tile, slots),
        in_specs=[vmem] * 2,
        out_specs=pl.BlockSpec(memory_space=pl.ANY),
        out_shape=jax.ShapeDtypeStruct((n_rows, n_cols), jnp.float32),
        scratch_shapes=[
            pltpu.VMEM((slots, tile, n_cols), jnp.float32),
            pltpu.SemaphoreType.DMA((slots,)),
        ],
        compiler_params=pltpu.CompilerParams(vmem_limit_bytes=20 << 20),
    )(left, right)


def per_device(density_slab, orbitals):
    left, right = factors(density_slab, orbitals)
    return outer(left, right, 1.0 / density_slab.shape[0])


def solution(mesh):
    return jax.shard_map(
        per_device,
        mesh=mesh,
        in_specs=(P("groups", "aux", "rep"), P(("groups", "rep"), "pts")),
        out_specs=P(("groups", "pts"), ("aux", "rep")),
        check_vma=False,
    )
```
